32 devices in a mesh: dp: 4 (over x, core), mp: 8 (over z, y).
Axes of the slice: x: 2, y: 2, z: 4, core: 2. Of those that a mesh axis runs over, the one named last changes fastest.
Arguments:
- hidden: bfloat16 [4, 4, 512, 2048], P('dp', None, None, 'mp'), may hold values from -6 to 6
- gain: float32 [2048], P('mp'), may hold values from 0.1 to 1.9
- cotangent: bfloat16 [4, 4, 512, 2048], P('dp', None, None, 'mp'), may hold values from -600 to 600
- blocks: int32 [4, 4, 2], P('dp'), may hold values from 1 to 2
- loss_mask: int32 [4, 4, 512], P('dp'), may hold values 0 or 1
- wi_gate: bfloat16 [5120, 2048], P('mp'), may hold values from -0.125 to 0.125
- wi_up: bfloat16 [5120, 2048], P('mp'), may hold values from -0.125 to 0.125
- wo_weight: bfloat16 [5120, 2048], P('mp'), may hold values from -0.078125 to 0.078125
Outputs:
- gradients: float32 [3, 5120, 2048], P(None, 'mp')
The draws below stay inside these ranges and needn't reach their ends.
Inputs may be any that keep to these rules, and one draw needn't show every extreme that they name: blocks of 128 target positions used by a sequence; later positions are padding.
All inputs are finite; a program needn't handle non-finite values. No bound on the sum of `loss_mask` on one device may be relied on, other than what follows from the above.
Results may differ from the reference program's by a relative error of at most 0.0059.
Values may be sent and summed in bfloat16 or wider, within the bound.
A program may use at most 128 MiB of HBM per device.

```python
import jax
import jax.numpy as jnp
from jax import lax

D = 2048
FF = 5120
MICRO = 4
BLOCK = 128
NBLK = 2
SEQ_MB = 2
GROUPS = 4
TLEN = 256
TOK_MB = 512


def place_ends(drawn, rng, low, high):
    extent = drawn.shape
    place = [jax.random.randint(jax.random.fold_in(rng, axis), (), 0, extent[axis]) for axis in range(len(extent))]
    drawn = drawn.at[tuple(place)].set(low)
    longest = extent.index(max(extent))
    place[longest] = (place[longest] + 1) % extent[longest]
    return drawn.at[tuple(place)].set(high)


def shard_levels(key, shape, pieces, least, top_value):
    def one(dim, shards_of):
        heights = jax.random.uniform(jax.random.fold_in(jax.random.fold_in(key, 6), dim), (shards_of,), jnp.float32, least / len(pieces), top_value / len(pieces))
        return jnp.repeat(jnp.exp(heights), shape[dim] // shards_of).reshape((-1,) + (1,) * (len(shape) - dim - 1))

    loudness = one(*pieces[0])
    for cut in pieces[1:]:
        loudness = loudness * one(*cut)
    return loudness


def normal_values(own_key, extent, width, reach, cuts=(), kind=jnp.bfloat16):
    values = width * jax.random.normal(own_key, extent, jnp.float32)
    if cuts:
        values = values * shard_levels(own_key, extent, cuts, -0.22, 0.18)
    return jnp.clip(values, -reach, reach).astype(kind)


def setup_inputs(seed: int = 0) -> dict:
    seeds = jax.random.split(jax.random.key(seed), 9)
    return {
        "hidden": normal_values(seeds[0], (GROUPS, MICRO, TOK_MB, D), 1.0, 6.0, ((0, 4), (3, 8))),
        "gain": jnp.clip(1.0 + 0.18 * jax.random.normal(seeds[1], (D,), jnp.float32), 0.1, 1.9),
        "cotangent": normal_values(seeds[2], (GROUPS, MICRO, TOK_MB, D), 100.0, 600.0, ((0, 4), (3, 8))),
        "blocks": place_ends(jax.random.randint(seeds[3], (GROUPS, MICRO, SEQ_MB), 1, NBLK + 1), jax.random.fold_in(seeds[3], 1), 1, NBLK).astype(jnp.int32),
        "loss_mask": place_ends((jax.random.randint(seeds[4], (GROUPS, MICRO, TOK_MB), 0, 4) < 3).astype(jnp.int32), jax.random.fold_in(seeds[4], 1), 0, 1),
        "wi_gate": normal_values(seeds[5], (FF, D), D ** -0.5, 0.125, ((0, 8),)),
        "wi_up": normal_values(seeds[6], (FF, D), D ** -0.5, 0.125, ((0, 8),)),
        "wo_weight": normal_values(seeds[7], (FF, D), FF ** -0.5, 0.078125, ((0, 8),)),
    }


def gelu_tanh(value):
    return jax.nn.gelu(value, approximate=True)

def contributions(normed, tangent, wi_gate, wi_up, wo_weight):
    rows_dims = (((1,), (1,)), ((), ()))
    gate_pre = lax.dot_general(normed, wi_gate, rows_dims, preferred_element_type=jnp.float32)
    up_pre = lax.dot_general(normed, wi_up, rows_dims, preferred_element_type=jnp.float32)
    activated, pullback = jax.vjp(gelu_tanh, gate_pre)
    inner = (activated * up_pre).astype(jnp.bfloat16)
    back_grad = lax.dot_general(tangent, wo_weight, rows_dims, preferred_element_type=jnp.float32)
    grad_gate = pullback(back_grad * up_pre)[0].astype(jnp.bfloat16)
    grad_up = (back_grad * activated).astype(jnp.bfloat16)
    dims = (((0,), (0,)), ((), ()))
    first_grad = lax.dot_general(grad_gate, normed, dims, preferred_element_type=jnp.float32)
    second_grad = lax.dot_general(grad_up, normed, dims, preferred_element_type=jnp.float32)
    third_grad = lax.dot_general(inner, tangent, dims, preferred_element_type=jnp.float32)
    return jnp.stack([first_grad, second_grad, third_grad])

def reference(hidden, gain, cotangent, blocks, loss_mask, wi_gate, wi_up, wo_weight):
    position = jnp.arange(TOK_MB, dtype=jnp.int32)
    offset = position % TLEN
    sequence = position // TLEN
    limit_pos = blocks[:, :, sequence] * BLOCK
    weight = (offset[None, None, :] < limit_pos).astype(jnp.int32) * loss_mask
    token_total = jnp.sum(weight)
    states = hidden.astype(jnp.float32)
    normed = (states * lax.rsqrt(lax.optimization_barrier(jnp.mean(states * states, axis=-1, keepdims=True)) + 1e-06) * gain).astype(jnp.bfloat16)
    tangent = cotangent * weight[..., None].astype(jnp.bfloat16)
    overall = jnp.zeros((3, FF, D), jnp.float32)
    for group_index in range(GROUPS):
        running_sum = jnp.zeros((3, FF, D), jnp.float32)
        compensation = jnp.zeros((3, FF, D), jnp.float32)
        for micro_step in range(MICRO):
            contrib = contributions(normed[group_index, micro_step], tangent[group_index, micro_step], wi_gate, wi_up, wo_weight)
            adjusted = contrib - compensation
            running = running_sum + adjusted
            compensation = running - running_sum - adjusted
            running_sum = running
        overall = overall + running_sum
    return overall / jnp.maximum(token_total, 1).astype(jnp.float32)
```

```python
import functools

import jax
import jax.numpy as jnp
from jax import lax
from jax.experimental import pallas as pl
from jax.experimental.pallas import tpu as pltpu
from jax.sharding import PartitionSpec as P

BLOCK = 128
TLEN = 256
MESH = pl.DeviceIdType.MESH


def ring_index(place, n):
    back = place // (n // 2)
    return (1 - back) * (2 * place) + back * (2 * (n - 1 - place) + 1)


def ring_place(index, n):
    odd = index % 2
    return (1 - odd) * (index // 2) + odd * (n - 1 - index // 2)


def gather_kernel(n, wide, h_ref, t_ref, hg_ref, tg_ref, local_sem, send_sem, recv_sem):
    micro, rows, cols = h_ref.shape
    me = lax.axis_index("mp")
    place = ring_place(me, n)
    ahead = ring_index(lax.rem(place + 1, n), n)
    behind = ring_index(lax.rem(place + n - 1, n), n)

    def spot(ref, owner, m):
        if wide:
            return ref.at[m, :, pl.ds(pl.multiple_of(owner * cols, cols), cols)]
        return ref.at[owner, m]

    barrier = pltpu.get_barrier_semaphore()
    for peer in (ahead, behind):
        pl.semaphore_signal(barrier, inc=1, device_id={"mp": peer}, device_id_type=MESH)
    pl.semaphore_wait(barrier, 2)

    own = []
    copies = {}
    for step in range(n - 1):
        for m in range(micro):
            for way, (src, dst, peer, sign) in enumerate(((h_ref, hg_ref, ahead, -1), (t_ref, tg_ref, behind, 1))):
                owner = ring_index(lax.rem(place + sign * step + n, n), n)
                if step > 0:
                    copies[step - 1, m, way].wait_recv()
                copy = pltpu.make_async_remote_copy(
                    src_ref=src.at[m] if step == 0 else spot(dst, owner, m),
                    dst_ref=spot(dst, owner, m),
                    send_sem=send_sem.at[way, step, m],
                    recv_sem=recv_sem.at[way, step, m],
                    device_id={"mp": peer},
                    device_id_type=MESH,
                )
                copy.start()
                copies[step, m, way] = copy
        if step == 0:
            for m in range(micro):
                for way, (src, dst) in enumerate(((h_ref, hg_ref), (t_ref, tg_ref))):
                    keep = pltpu.make_async_copy(src.at[m], spot(dst, me, m), local_sem.at[way, m])
                    keep.start()
                    own.append(keep)
    for (step, m, way), copy in copies.items():
        copy.wait_send()
        if step == n - 2:
            copy.wait_recv()
    for keep in own:
        keep.wait()


def gather_rows(hidden, tangent, n):
    micro, rows, cols = hidden.shape
    wide = cols % 128 == 0
    shape = (micro, rows, n * cols) if wide else (n, micro, rows, cols)
    hg, tg = pl.pallas_call(
        functools.partial(gather_kernel, n, wide),
        out_shape=[jax.ShapeDtypeStruct(shape, hidden.dtype)] * 2,
        in_specs=[pl.BlockSpec(memory_space=pl.ANY)] * 2,
        out_specs=[pl.BlockSpec(memory_space=pl.ANY)] * 2,
        scratch_shapes=[
            pltpu.SemaphoreType.DMA((2, micro)),
            pltpu.SemaphoreType.DMA((2, n - 1, micro)),
            pltpu.SemaphoreType.DMA((2, n - 1, micro)),
        ],
        compiler_params=pltpu.CompilerParams(collective_id=0, has_side_effects=True),
        name="gather_rows",
    )(hidden, tangent)
    if not wide:
        hg, tg = (jnp.transpose(a, (1, 2, 0, 3)).reshape(micro, rows, n * cols) for a in (hg, tg))
    return hg, tg


def gelu_tanh(value):
    return jax.nn.gelu(value, approximate=True)


def factors(normed, tangent, wi_gate, wi_up, wo_weight):
    rows_dims = (((1,), (1,)), ((), ()))
    gate_pre = lax.dot_general(normed, wi_gate, rows_dims, preferred_element_type=jnp.float32)
    up_pre = lax.dot_general(normed, wi_up, rows_dims, preferred_element_type=jnp.float32)
    activated, pullback = jax.vjp(gelu_tanh, gate_pre)
    inner = (activated * up_pre).astype(jnp.bfloat16)
    back_grad = lax.dot_general(tangent, wo_weight, rows_dims, preferred_element_type=jnp.float32)
    grad_gate = pullback(back_grad * up_pre)[0].astype(jnp.bfloat16)
    grad_up = (back_grad * activated).astype(jnp.bfloat16)
    return grad_gate, grad_up, inner


def kahan(pairs):
    dims = (((0,), (0,)), ((), ()))
    total = comp = None
    for left, right in pairs:
        term = lax.dot_general(left, right, dims, preferred_element_type=jnp.float32)
        if total is None:
            total, comp = term, jnp.zeros_like(term)
            continue
        adjusted = term - comp
        running = total + adjusted
        comp = running - total - adjusted
        total = running
    return total


def swap(value, bit, size):
    return lax.ppermute(value, "dp", [(i, i ^ bit) for i in range(size)])


def reduce_groups(total, denominator, size):
    core = lax.axis_index("dp") % 2
    half = total.shape[1] // 2
    give = lax.dynamic_slice_in_dim(total, (1 - core) * half, half, 1).astype(jnp.bfloat16)
    keep = lax.dynamic_slice_in_dim(total, core * half, half, 1)
    part = keep + swap(give, 1, size).astype(jnp.float32)
    bit = 2
    while bit < size:
        mine = part.astype(jnp.bfloat16)
        part = mine.astype(jnp.float32) + swap(mine, bit, size).astype(jnp.float32)
        bit *= 2
    mine = (part / denominator).astype(jnp.bfloat16)
    theirs = swap(mine, 1, size)
    low = jnp.where(core == 0, mine, theirs)
    high = jnp.where(core == 0, theirs, mine)
    return jnp.concatenate([low, high], axis=1).astype(jnp.float32)


def on_device(n, groups, hidden, gain, cotangent, blocks, loss_mask, wi_gate, wi_up, wo_weight):
    row_count = hidden.shape[2]
    micro_count = hidden.shape[1]
    position = lax.iota(jnp.int32, row_count)
    offset = position % TLEN
    sequence = position // TLEN
    picker = (sequence[None, :] == lax.iota(jnp.int32, blocks.shape[2])[:, None]).astype(jnp.int32)
    limit_pos = jnp.sum(blocks[0][:, :, None] * picker[None, :, :], axis=1) * BLOCK
    weight = (offset[None, :] < limit_pos).astype(jnp.int32) * loss_mask[0]
    token_total = lax.psum(jnp.sum(weight), "dp")
    denominator = jnp.maximum(token_total, 1).astype(jnp.float32)
    whole_gain = lax.all_gather(gain, "mp", axis=0, tiled=True)
    tangent = cotangent[0] * weight[:, :, None].astype(jnp.bfloat16)
    states, whole_tangent = gather_rows(hidden[0], tangent, n)
    states = states.astype(jnp.float32)
    squares = jnp.mean(states * states, axis=-1, keepdims=True)
    normed = (states * lax.rsqrt(squares + 1e-06) * whole_gain).astype(jnp.bfloat16)
    made = [factors(normed[m], whole_tangent[m], wi_gate, wi_up, wo_weight) for m in range(micro_count)]
    results = []
    for which in (2, 1, 0):
        right = whole_tangent if which == 2 else normed
        total = kahan([(made[m][which], right[m]) for m in range(micro_count)])
        results.append(reduce_groups(total, denominator, groups))
    return jnp.stack(results[::-1])


def solution(mesh):
    return jax.shard_map(
        functools.partial(on_device, mesh.shape["mp"], mesh.shape["dp"]),
        mesh=mesh,
        in_specs=(
            P("dp", None, None, "mp"),
            P("mp"),
            P("dp", None, None, "mp"),
            P("dp", None, None),
            P("dp", None, None),
            P("mp", None),
            P("mp", None),
            P("mp", None),
        ),
        out_specs=P(None, "mp", None),
        check_vma=False,
    )
```

```python
import functools

import jax
import jax.numpy as jnp
from jax import lax
from jax.experimental import pallas as pl
from jax.experimental.pallas import tpu as pltpu
from jax.sharding import PartitionSpec as P

BLOCK = 128
TLEN = 256
MESH = pl.DeviceIdType.MESH


def ring_index(place, n):
    back = place // (n // 2)
    return (1 - back) * (2 * place) + back * (2 * (n - 1 - place) + 1)


def ring_place(index, n):
    odd = index % 2
    return (1 - odd) * (index // 2) + odd * (n - 1 - index // 2)


def gather_kernel(n, wide, h_ref, t_ref, g_ref, hg_ref, tg_ref, gg_ref, local_sem, send_sem, recv_sem, gain_sem):
    micro, rows, cols = h_ref.shape
    me = lax.axis_index("mp")
    place = ring_place(me, n)
    ahead = ring_index(lax.rem(place + 1, n), n)
    behind = ring_index(lax.rem(place + n - 1, n), n)

    def spot(ref, owner, m):
        if wide:
            return ref.at[m, :, pl.ds(pl.multiple_of(owner * cols, cols), cols)]
        return ref.at[owner, m]

    barrier = pltpu.get_barrier_semaphore()
    for peer in (ahead, behind):
        pl.semaphore_signal(barrier, inc=1, device_id={"mp": peer}, device_id_type=MESH)
    pl.semaphore_wait(barrier, 2)

    own = []
    copies = {}
    for step in range(n - 1):
        owner = ring_index(lax.rem(place - step + n, n), n)
        if step > 0:
            copies[step - 1, 0, 2].wait_recv()
        copies[step, 0, 2] = pltpu.make_async_remote_copy(
            src_ref=g_ref if step == 0 else gg_ref.at[owner],
            dst_ref=gg_ref.at[owner],
            send_sem=gain_sem.at[1, step],
            recv_sem=gain_sem.at[2, step],
            device_id={"mp": ahead},
            device_id_type=MESH,
        )
        copies[step, 0, 2].start()
        for m in range(micro):
            for way, (src, dst, peer, sign) in enumerate(((h_ref, hg_ref, ahead, -1), (t_ref, tg_ref, behind, 1))):
                owner = ring_index(lax.rem(place + sign * step + n, n), n)
                if step > 0:
                    copies[step - 1, m, way].wait_recv()
                copy = pltpu.make_async_remote_copy(
                    src_ref=src.at[m] if step == 0 else spot(dst, owner, m),
                    dst_ref=spot(dst, owner, m),
                    send_sem=send_sem.at[way, step, m],
                    recv_sem=recv_sem.at[way, step, m],
                    device_id={"mp": peer},
                    device_id_type=MESH,
                )
                copy.start()
                copies[step, m, way] = copy
        if step == 0:
            own.append(pltpu.make_async_copy(g_ref, gg_ref.at[me], gain_sem.at[0, 0]))
            for m in range(micro):
                for way, (src, dst) in enumerate(((h_ref, hg_ref), (t_ref, tg_ref))):
                    own.append(pltpu.make_async_copy(src.at[m], spot(dst, me, m), local_sem.at[way, m]))
            for keep in own:
                keep.start()
    for (step, m, way), copy in copies.items():
        copy.wait_send()
        if step == n - 2:
            copy.wait_recv()
    for keep in own:
        keep.wait()


def gather_rows(hidden, tangent, gain, n, ident):
    micro, rows, cols = hidden.shape
    wide = cols % 128 == 0
    shape = (micro, rows, n * cols) if wide else (n, micro, rows, cols)
    hg, tg, gg = pl.pallas_call(
        functools.partial(gather_kernel, n, wide),
        out_shape=[jax.ShapeDtypeStruct(shape, hidden.dtype)] * 2 + [jax.ShapeDtypeStruct((n, 1, cols), gain.dtype)],
        in_specs=[pl.BlockSpec(memory_space=pl.ANY)] * 3,
        out_specs=[pl.BlockSpec(memory_space=pl.ANY)] * 3,
        scratch_shapes=[
            pltpu.SemaphoreType.DMA((2, micro)),
            pltpu.SemaphoreType.DMA((2, n - 1, micro)),
            pltpu.SemaphoreType.DMA((2, n - 1, micro)),
            pltpu.SemaphoreType.DMA((3, n - 1)),
        ],
        compiler_params=pltpu.CompilerParams(collective_id=ident, has_side_effects=True),
        name=f"gather_rows_{ident}",
    )(hidden, tangent, gain[None])
    if not wide:
        hg, tg = (jnp.transpose(a, (1, 2, 0, 3)).reshape(micro, rows, n * cols) for a in (hg, tg))
    return hg, tg, gg.reshape(n * cols)


def gelu_tanh(value):
    return jax.nn.gelu(value, approximate=True)


def factors(normed, tangent, wi_gate, wi_up, wo_weight):
    rows_dims = (((1,), (1,)), ((), ()))
    gate_pre = lax.dot_general(normed, wi_gate, rows_dims, preferred_element_type=jnp.float32)
    up_pre = lax.dot_general(normed, wi_up, rows_dims, preferred_element_type=jnp.float32)
    activated, pullback = jax.vjp(gelu_tanh, gate_pre)
    inner = (activated * up_pre).astype(jnp.bfloat16)
    back_grad = lax.dot_general(tangent, wo_weight, rows_dims, preferred_element_type=jnp.float32)
    grad_gate = pullback(back_grad * up_pre)[0].astype(jnp.bfloat16)
    grad_up = (back_grad * activated).astype(jnp.bfloat16)
    return grad_gate, grad_up, inner


def kahan(pairs):
    dims = (((0,), (0,)), ((), ()))
    total = comp = None
    for left, right in pairs:
        term = lax.dot_general(left, right, dims, preferred_element_type=jnp.float32)
        if total is None:
            total, comp = term, jnp.zeros_like(term)
            continue
        adjusted = term - comp
        running = total + adjusted
        comp = running - total - adjusted
        total = running
    return total


def swap(value, bit, size):
    return lax.ppermute(value, "dp", [(i, i ^ bit) for i in range(size)])


def core_half(total, size):
    core = lax.axis_index("dp") % 2
    half = total.shape[1] // 2
    give = lax.dynamic_slice_in_dim(total, (1 - core) * half, half, 1).astype(jnp.bfloat16)
    keep = lax.dynamic_slice_in_dim(total, core * half, half, 1)
    return keep + swap(give, 1, size).astype(jnp.float32)


def over_groups(mine, denominator, size):
    core = lax.axis_index("dp") % 2
    bit = 2
    while bit < size:
        part = mine.astype(jnp.float32) + swap(mine, bit, size).astype(jnp.float32)
        bit *= 2
        mine = part.astype(jnp.bfloat16) if bit < size else (part / denominator).astype(jnp.bfloat16)
    theirs = swap(mine, 1, size)
    low = jnp.where(core == 0, mine, theirs)
    high = jnp.where(core == 0, theirs, mine)
    return jnp.concatenate([low, high], axis=1).astype(jnp.float32)


def gradients(n, groups, ident, hidden, tangent, gain, denominator, wi_gate, wi_up, wo_weight):
    states, whole_tangent, whole_gain = gather_rows(hidden, tangent, gain, n, ident)
    states = states.astype(jnp.float32)
    squares = jnp.mean(states * states, axis=-1, keepdims=True)
    normed = (states * lax.rsqrt(squares + 1e-06) * whole_gain).astype(jnp.bfloat16)
    steps = range(hidden.shape[0])
    made = [factors(normed[m], whole_tangent[m], wi_gate, wi_up, wo_weight) for m in steps]
    units = wi_gate.shape[0]
    middle = (units // 128 + 1) // 2 * 128
    cuts = [0, middle, units] if 0 < middle < units else [0, units]
    jobs = [(which, low, high) for which in (2, 1, 0) for low, high in zip(cuts[:-1], cuts[1:])]
    sent = []
    for spot, (which, low, high) in enumerate(jobs):
        lefts = [made[m][which][:, low:high] for m in steps]
        if spot >= 2:
            lefts, sent[spot - 2] = lax.optimization_barrier((lefts, sent[spot - 2]))
        right = whole_tangent if which == 2 else normed
        total = kahan([(lefts[m], right[m]) for m in steps])
        sent.append(core_half(total, groups).astype(jnp.bfloat16))
    parts = [over_groups(mine, denominator, groups) for mine in sent]
    each = len(cuts) - 1
    kinds = [jnp.concatenate(parts[k * each : (k + 1) * each], axis=0) for k in (2, 1, 0)]
    return jnp.stack(kinds)


def on_device(n, groups, hidden, gain, cotangent, blocks, loss_mask, wi_gate, wi_up, wo_weight):
    _, micro_count, row_count, cols = hidden.shape
    position = lax.iota(jnp.int32, row_count)
    offset = position % TLEN
    sequence = position // TLEN
    picker = (sequence[None, :] == lax.iota(jnp.int32, blocks.shape[2])[:, None]).astype(jnp.int32)
    limit_pos = jnp.sum(blocks[0][:, :, None] * picker[None, :, :], axis=1) * BLOCK
    weight = (offset[None, :] < limit_pos).astype(jnp.int32) * loss_mask[0]
    mine = (lax.iota(jnp.int32, groups) == lax.axis_index("dp")).astype(jnp.int32)
    counts = lax.psum(jnp.sum(weight) * mine, "dp")
    denominator = jnp.maximum(jnp.sum(counts), 1).astype(jnp.float32)
    room = row_count * 3 // 4
    weights = (wi_gate, wi_up, wo_weight)

    def packed(_):
        lines = weight.reshape(-1, 128)
        lane = lax.iota(jnp.int32, 128)
        within = jnp.sum(lines[:, :, None] * (lane[:, None] < lane[None, :]), axis=1)
        line = lax.iota(jnp.int32, lines.shape[0])
        before = jnp.sum(jnp.sum(lines, axis=1)[:, None] * (line[:, None] < line[None, :]), axis=0)
        target = jnp.where(lines > 0, within + before[:, None], -1).reshape(-1)
        pick = (lax.iota(jnp.int32, micro_count * room)[:, None] == target[None, :]).astype(jnp.bfloat16)
        both = [
            jnp.dot(pick, a[0].reshape(-1, cols), preferred_element_type=jnp.float32).astype(a.dtype).reshape(micro_count, room, cols)
            for a in (hidden, cotangent)
        ]
        return gradients(n, groups, 1, *both, gain, denominator, *weights)

    def whole(_):
        tangent = cotangent[0] * weight[:, :, None].astype(jnp.bfloat16)
        return gradients(n, groups, 0, hidden[0], tangent, gain, denominator, *weights)

    return lax.cond(jnp.max(counts) <= micro_count * room, packed, whole, 0)


def solution(mesh):
    return jax.shard_map(
        functools.partial(on_device, mesh.shape["mp"], mesh.shape["dp"]),
        mesh=mesh,
        in_specs=(
            P("dp", None, None, "mp"),
            P("mp"),
            P("dp", None, None, "mp"),
            P("dp", None, None),
            P("dp", None, None),
            P("mp", None),
            P("mp", None),
            P("mp", None),
        ),
        out_specs=P(None, "mp", None),
        check_vma=False,
    )
```

```python
import functools

import jax
import jax.numpy as jnp
from jax import lax
from jax.experimental import pallas as pl
from jax.experimental.pallas import tpu as pltpu
from jax.sharding import PartitionSpec as P

BLOCK = 128
TLEN = 256
MESH = pl.DeviceIdType.MESH


def ring_index(place, n):
    back = place // (n // 2)
    return (1 - back) * (2 * place) + back * (2 * (n - 1 - place) + 1)


def ring_place(index, n):
    odd = index % 2
    return (1 - odd) * (index // 2) + odd * (n - 1 - index // 2)


def gather_kernel(n, wide, h_ref, t_ref, g_ref, hg_ref, tg_ref, gg_ref, local_sem, send_sem, recv_sem, gain_sem):
    micro, rows, cols = h_ref.shape
    me = lax.axis_index("mp")
    place = ring_place(me, n)
    ahead = ring_index(lax.rem(place + 1, n), n)
    behind = ring_index(lax.rem(place + n - 1, n), n)

    def spot(ref, owner, m):
        if wide:
            return ref.at[m, :, pl.ds(pl.multiple_of(owner * cols, cols), cols)]
        return ref.at[owner, m]

    barrier = pltpu.get_barrier_semaphore()
    for peer in (ahead, behind):
        pl.semaphore_signal(barrier, inc=1, device_id={"mp": peer}, device_id_type=MESH)
    pl.semaphore_wait(barrier, 2)

    own = []
    copies = {}
    for step in range(n - 1):
        owner = ring_index(lax.rem(place - step + n, n), n)
        if step > 0:
            copies[step - 1, 0, 2].wait_recv()
        copies[step, 0, 2] = pltpu.make_async_remote_copy(
            src_ref=g_ref if step == 0 else gg_ref.at[owner],
            dst_ref=gg_ref.at[owner],
            send_sem=gain_sem.at[1, step],
            recv_sem=gain_sem.at[2, step],
            device_id={"mp": ahead},
            device_id_type=MESH,
        )
        copies[step, 0, 2].start()
        for m in range(micro):
            for way, (src, dst, peer, sign) in enumerate(((h_ref, hg_ref, ahead, -1), (t_ref, tg_ref, behind, 1))):
                owner = ring_index(lax.rem(place + sign * step + n, n), n)
                if step > 0:
                    copies[step - 1, m, way].wait_recv()
                copy = pltpu.make_async_remote_copy(
                    src_ref=src.at[m] if step == 0 else spot(dst, owner, m),
                    dst_ref=spot(dst, owner, m),
                    send_sem=send_sem.at[way, step, m],
                    recv_sem=recv_sem.at[way, step, m],
                    device_id={"mp": peer},
                    device_id_type=MESH,
                )
                copy.start()
                copies[step, m, way] = copy
        if step == 0:
            own.append(pltpu.make_async_copy(g_ref, gg_ref.at[me], gain_sem.at[0, 0]))
            for m in range(micro):
                for way, (src, dst) in enumerate(((h_ref, hg_ref), (t_ref, tg_ref))):
                    own.append(pltpu.make_async_copy(src.at[m], spot(dst, me, m), local_sem.at[way, m]))
            for keep in own:
                keep.start()
    for (step, m, way), copy in copies.items():
        copy.wait_send()
        if step == n - 2:
            copy.wait_recv()
    for keep in own:
        keep.wait()


def gather_rows(hidden, tangent, gain, n, ident):
    micro, rows, cols = hidden.shape
    wide = cols % 128 == 0
    shape = (micro, rows, n * cols) if wide else (n, micro, rows, cols)
    hg, tg, gg = pl.pallas_call(
        functools.partial(gather_kernel, n, wide),
        out_shape=[jax.ShapeDtypeStruct(shape, hidden.dtype)] * 2 + [jax.ShapeDtypeStruct((n, 1, cols), gain.dtype)],
        in_specs=[pl.BlockSpec(memory_space=pl.ANY)] * 3,
        out_specs=[pl.BlockSpec(memory_space=pl.ANY)] * 3,
        scratch_shapes=[
            pltpu.SemaphoreType.DMA((2, micro)),
            pltpu.SemaphoreType.DMA((2, n - 1, micro)),
            pltpu.SemaphoreType.DMA((2, n - 1, micro)),
            pltpu.SemaphoreType.DMA((3, n - 1)),
        ],
        compiler_params=pltpu.CompilerParams(collective_id=ident, has_side_effects=True),
        name=f"gather_rows_{ident}",
    )(hidden, tangent, gain[None])
    if not wide:
        hg, tg = (jnp.transpose(a, (1, 2, 0, 3)).reshape(micro, rows, n * cols) for a in (hg, tg))
    return hg, tg, gg.reshape(n * cols)


def gelu_tanh(value):
    return jax.nn.gelu(value, approximate=True)


def rows_product(rows, units):
    return lax.dot_general(rows, units, (((1,), (1,)), ((), ())), preferred_element_type=jnp.float32)


def kahan(pairs):
    dims = (((0,), (0,)), ((), ()))
    total = comp = None
    for left, right in pairs:
        term = lax.dot_general(left, right, dims, preferred_element_type=jnp.float32)
        if total is None:
            total, comp = term, jnp.zeros_like(term)
            continue
        adjusted = term - comp
        running = total + adjusted
        comp = running - total - adjusted
        total = running
    return total


def swap(value, bit, size):
    return lax.ppermute(value, "dp", [(i, i ^ bit) for i in range(size)])


def core_half(total, size):
    core = lax.axis_index("dp") % 2
    half = total.shape[1] // 2
    give = lax.dynamic_slice_in_dim(total, (1 - core) * half, half, 1).astype(jnp.bfloat16)
    keep = lax.dynamic_slice_in_dim(total, core * half, half, 1)
    return keep + swap(give, 1, size).astype(jnp.float32)


def over_groups(mine, denominator, size):
    core = lax.axis_index("dp") % 2
    bit = 2
    while bit < size:
        part = mine.astype(jnp.float32) + swap(mine, bit, size).astype(jnp.float32)
        bit *= 2
        mine = part.astype(jnp.bfloat16) if bit < size else (part / denominator).astype(jnp.bfloat16)
    theirs = swap(mine, 1, size)
    low = jnp.where(core == 0, mine, theirs)
    high = jnp.where(core == 0, theirs, mine)
    return low, high


def gradients(n, groups, ident, hidden, tangent, gain, denominator, wi_gate, wi_up, wo_weight):
    states, whole_tangent, whole_gain = gather_rows(hidden, tangent, gain, n, ident)
    states = states.astype(jnp.float32)
    squares = jnp.mean(states * states, axis=-1, keepdims=True)
    normed = (states * lax.rsqrt(squares + 1e-06) * whole_gain).astype(jnp.bfloat16)
    steps = range(hidden.shape[0])
    units = wi_gate.shape[0]
    middle = (units // 128 + 1) // 2 * 128
    cuts = [0, middle, units] if 0 < middle < units else [0, units]
    sent, spots = [], []

    def job(which, low, lefts, rights):
        if len(sent) >= 2:
            lefts, sent[-2] = lax.optimization_barrier((lefts, sent[-2]))
        total = kahan(list(zip(lefts, rights)))
        sent.append(core_half(total, groups).astype(jnp.bfloat16))
        spots.append((which, low))
        return total

    normed = [normed[m] for m in steps]
    masked = [whole_tangent[m] for m in steps]
    for low, high in zip(cuts[:-1], cuts[1:]):
        gate_rows, up_rows, out_rows = (w[low:high] for w in (wi_gate, wi_up, wo_weight))
        if sent:
            gate_rows, up_rows, sent[-2] = lax.optimization_barrier((gate_rows, up_rows, sent[-2]))
        up_pre = [rows_product(normed[m], up_rows) for m in steps]
        pulls = [jax.vjp(gelu_tanh, rows_product(normed[m], gate_rows)) for m in steps]
        inner = [(pulls[m][0] * up_pre[m]).astype(jnp.bfloat16) for m in steps]
        total = job(2, low, inner, masked)
        out_rows, _ = lax.optimization_barrier((out_rows, total))
        back_grad = [rows_product(masked[m], out_rows) for m in steps]
        grad_up = [(back_grad[m] * pulls[m][0]).astype(jnp.bfloat16) for m in steps]
        job(1, low, grad_up, normed)
        grad_gate = [pulls[m][1](back_grad[m] * up_pre[m])[0].astype(jnp.bfloat16) for m in steps]
        job(0, low, grad_gate, normed)
    result = jnp.zeros((3,) + wi_gate.shape, jnp.float32)
    for mine, (which, low) in zip(sent, spots):
        halves = over_groups(mine, denominator, groups)
        for side, half in enumerate(halves):
            result = lax.dynamic_update_slice(result, half[None].astype(jnp.float32), (which, low, side * half.shape[1]))
    return result


def on_device(n, groups, hidden, gain, cotangent, blocks, loss_mask, wi_gate, wi_up, wo_weight):
    _, micro_count, row_count, cols = hidden.shape
    position = lax.iota(jnp.int32, row_count)
    offset = position % TLEN
    sequence = position // TLEN
    picker = (sequence[None, :] == lax.iota(jnp.int32, blocks.shape[2])[:, None]).astype(jnp.int32)
    limit_pos = jnp.sum(blocks[0][:, :, None] * picker[None, :, :], axis=1) * BLOCK
    weight = (offset[None, :] < limit_pos).astype(jnp.int32) * loss_mask[0]
    mine = (lax.iota(jnp.int32, groups) == lax.axis_index("dp")).astype(jnp.int32)
    counts = lax.psum(jnp.sum(weight) * mine, "dp")
    denominator = jnp.maximum(jnp.sum(counts), 1).astype(jnp.float32)
    room = row_count * 3 // 4
    weights = (wi_gate, wi_up, wo_weight)

    def packed(_):
        lines = weight.reshape(-1, 128)
        lane = lax.iota(jnp.int32, 128)
        within = jnp.sum(lines[:, :, None] * (lane[:, None] < lane[None, :]), axis=1)
        line = lax.iota(jnp.int32, lines.shape[0])
        before = jnp.sum(jnp.sum(lines, axis=1)[:, None] * (line[:, None] < line[None, :]), axis=0)
        target = jnp.where(lines > 0, within + before[:, None], -1).reshape(-1)
        pick = (lax.iota(jnp.int32, micro_count * room)[:, None] == target[None, :]).astype(jnp.bfloat16)
        both = [
            jnp.dot(pick, a[0].reshape(-1, cols), preferred_element_type=jnp.float32).astype(a.dtype).reshape(micro_count, room, cols)
            for a in (hidden, cotangent)
        ]
        return gradients(n, groups, 1, *both, gain, denominator, *weights)

    def whole(_):
        tangent = cotangent[0] * weight[:, :, None].astype(jnp.bfloat16)
        return gradients(n, groups, 0, hidden[0], tangent, gain, denominator, *weights)

    return lax.cond(jnp.max(counts) <= micro_count * room, packed, whole, 0)


def solution(mesh):
    return jax.shard_map(
        functools.partial(on_device, mesh.shape["mp"], mesh.shape["dp"]),
        mesh=mesh,
        in_specs=(
            P("dp", None, None, "mp"),
            P("mp"),
            P("dp", None, None, "mp"),
            P("dp", None, None),
            P("dp", None, None),
            P("mp", None),
            P("mp", None),
            P("mp", None),
        ),
        out_specs=P(None, "mp", None),
        check_vma=False,
    )
```

```python
import functools

import jax
import jax.numpy as jnp
from jax import lax
from jax.experimental import pallas as pl
from jax.experimental.pallas import tpu as pltpu
from jax.sharding import PartitionSpec as P

BLOCK = 128
TLEN = 256
MESH = pl.DeviceIdType.MESH


def ring_index(place, n):
    back = place // (n // 2)
    return (1 - back) * (2 * place) + back * (2 * (n - 1 - place) + 1)


def ring_place(index, n):
    odd = index % 2
    return (1 - odd) * (index // 2) + odd * (n - 1 - index // 2)


def gather_kernel(n, wide, h_ref, t_ref, g_ref, hg_ref, tg_ref, gg_ref, local_sem, send_sem, recv_sem, gain_sem):
    micro, rows, cols = h_ref.shape
    me = lax.axis_index("mp")
    place = ring_place(me, n)
    ahead = ring_index(lax.rem(place + 1, n), n)
    behind = ring_index(lax.rem(place + n - 1, n), n)

    def spot(ref, owner, m):
        if wide:
            return ref.at[m, :, pl.ds(pl.multiple_of(owner * cols, cols), cols)]
        return ref.at[owner, m]

    barrier = pltpu.get_barrier_semaphore()
    for peer in (ahead, behind):
        pl.semaphore_signal(barrier, inc=1, device_id={"mp": peer}, device_id_type=MESH)
    pl.semaphore_wait(barrier, 2)

    own = []
    copies = {}
    for step in range(n - 1):
        owner = ring_index(lax.rem(place - step + n, n), n)
        if step > 0:
            copies[step - 1, 0, 2].wait_recv()
        copies[step, 0, 2] = pltpu.make_async_remote_copy(
            src_ref=g_ref if step == 0 else gg_ref.at[owner],
            dst_ref=gg_ref.at[owner],
            send_sem=gain_sem.at[1, step],
            recv_sem=gain_sem.at[2, step],
            device_id={"mp": ahead},
            device_id_type=MESH,
        )
        copies[step, 0, 2].start()
        for m in range(micro):
            for way, (src, dst, peer, sign) in enumerate(((h_ref, hg_ref, ahead, -1), (t_ref, tg_ref, behind, 1))):
                owner = ring_index(lax.rem(place + sign * step + n, n), n)
                if step > 0:
                    copies[step - 1, m, way].wait_recv()
                copy = pltpu.make_async_remote_copy(
                    src_ref=src.at[m] if step == 0 else spot(dst, owner, m),
                    dst_ref=spot(dst, owner, m),
                    send_sem=send_sem.at[way, step, m],
                    recv_sem=recv_sem.at[way, step, m],
                    device_id={"mp": peer},
                    device_id_type=MESH,
                )
                copy.start()
                copies[step, m, way] = copy
        if step == 0:
            own.append(pltpu.make_async_copy(g_ref, gg_ref.at[me], gain_sem.at[0, 0]))
            for m in range(micro):
                for way, (src, dst) in enumerate(((h_ref, hg_ref), (t_ref, tg_ref))):
                    own.append(pltpu.make_async_copy(src.at[m], spot(dst, me, m), local_sem.at[way, m]))
            for keep in own:
                keep.start()
    for (step, m, way), copy in copies.items():
        copy.wait_send()
        if step == n - 2:
            copy.wait_recv()
    for keep in own:
        keep.wait()


def gather_rows(hidden, tangent, gain, n, ident):
    micro, rows, cols = hidden.shape
    wide = cols % 128 == 0
    shape = (micro, rows, n * cols) if wide else (n, micro, rows, cols)
    hg, tg, gg = pl.pallas_call(
        functools.partial(gather_kernel, n, wide),
        out_shape=[jax.ShapeDtypeStruct(shape, hidden.dtype)] * 2 + [jax.ShapeDtypeStruct((n, 1, cols), gain.dtype)],
        in_specs=[pl.BlockSpec(memory_space=pl.ANY)] * 3,
        out_specs=[pl.BlockSpec(memory_space=pl.ANY)] * 3,
        scratch_shapes=[
            pltpu.SemaphoreType.DMA((2, micro)),
            pltpu.SemaphoreType.DMA((2, n - 1, micro)),
            pltpu.SemaphoreType.DMA((2, n - 1, micro)),
            pltpu.SemaphoreType.DMA((3, n - 1)),
        ],
        compiler_params=pltpu.CompilerParams(collective_id=ident, has_side_effects=True),
        name=f"gather_rows_{ident}",
    )(hidden, tangent, gain[None])
    if not wide:
        hg, tg = (jnp.transpose(a, (1, 2, 0, 3)).reshape(micro, rows, n * cols) for a in (hg, tg))
    return hg, tg, gg.reshape(n * cols)


def gelu_tanh(value):
    return jax.nn.gelu(value, approximate=True)


def rows_product(rows, units):
    return lax.dot_general(rows, units, (((1,), (1,)), ((), ())), preferred_element_type=jnp.float32)


def kahan(pairs):
    dims = (((0,), (0,)), ((), ()))
    total = comp = None
    for left, right in pairs:
        term = lax.dot_general(left, right, dims, preferred_element_type=jnp.float32)
        if total is None:
            total, comp = term, jnp.zeros_like(term)
            continue
        adjusted = term - comp
        running = total + adjusted
        comp = running - total - adjusted
        total = running
    return total


def swap(value, bit, size):
    return lax.ppermute(value, "dp", [(i, i ^ bit) for i in range(size)])


def core_halves(total):
    core = lax.axis_index("dp") % 2
    half = total.shape[1] // 2
    give = lax.dynamic_slice_in_dim(total, (1 - core) * half, half, 1).astype(jnp.bfloat16)
    keep = lax.dynamic_slice_in_dim(total, core * half, half, 1)
    return give, keep


def over_groups(mine, size):
    bit = 2
    while bit * 2 < size:
        mine = (mine.astype(jnp.float32) + swap(mine, bit, size).astype(jnp.float32)).astype(jnp.bfloat16)
        bit *= 2
    return mine, swap(mine, bit, size)


def gradients(n, groups, ident, hidden, tangent, gain, denominator, wi_gate, wi_up, wo_weight):
    states, whole_tangent, whole_gain = gather_rows(hidden, tangent, gain, n, ident)
    states = states.astype(jnp.float32)
    squares = jnp.mean(states * states, axis=-1, keepdims=True)
    normed = (states * lax.rsqrt(squares + 1e-06) * whole_gain).astype(jnp.bfloat16)
    steps = range(hidden.shape[0])
    units = wi_gate.shape[0]
    middle = (units // 128 + 1) // 2 * 128
    cuts = [0, middle, units] if 0 < middle < units else [0, units]
    sent, spots = [], []

    def job(which, low, lefts, rights, after):
        if after < len(sent):
            lefts, sent[after] = lax.optimization_barrier((lefts, sent[after]))
        give, keep = core_halves(kahan(list(zip(lefts, rights))))
        sent.append((keep + swap(give, 1, groups).astype(jnp.float32)).astype(jnp.bfloat16))
        spots.append((which, low))
        return give

    normed = [normed[m] for m in steps]
    masked = [whole_tangent[m] for m in steps]
    for low, high in zip(cuts[:-1], cuts[1:]):
        gate_rows, up_rows, out_rows = (w[low:high] for w in (wi_gate, wi_up, wo_weight))
        if sent:
            gate_rows, up_rows, sent[-2] = lax.optimization_barrier((gate_rows, up_rows, sent[-2]))
        up_pre = [rows_product(normed[m], up_rows) for m in steps]
        pulls = [jax.vjp(gelu_tanh, rows_product(normed[m], gate_rows)) for m in steps]
        inner = [(pulls[m][0] * up_pre[m]).astype(jnp.bfloat16) for m in steps]
        give = job(2, low, inner, masked, max(len(sent) - 2, 0))
        out_rows, _ = lax.optimization_barrier((out_rows, give))
        back_grad = [rows_product(masked[m], out_rows) for m in steps]
        grad_up = [(back_grad[m] * pulls[m][0]).astype(jnp.bfloat16) for m in steps]
        job(1, low, grad_up, normed, len(sent) - 1)
        grad_gate = [pulls[m][1](back_grad[m] * up_pre[m])[0].astype(jnp.bfloat16) for m in steps]
        job(0, low, grad_gate, normed, len(sent) - 2)
    result = jnp.zeros((3,) + wi_gate.shape, jnp.float32)
    result, sent[-1] = lax.optimization_barrier((result, sent[-1]))
    core = lax.axis_index("dp") % 2
    crossing = [over_groups(mine, groups) for mine in sent]
    done = []
    for spot, (mine, other) in enumerate(crossing):
        if spot >= 2:
            result = place_halves(result, done[spot - 2], spots[spot - 2], core)
            result, other = lax.optimization_barrier((result, other))
        mine = ((mine.astype(jnp.float32) + other.astype(jnp.float32)) / denominator).astype(jnp.bfloat16)
        done.append((mine, swap(mine, 1, groups)))
    for pair, where in list(zip(done, spots))[-2:]:
        result = place_halves(result, pair, where, core)
    return result


def place_halves(result, pair, where, core):
    mine, theirs = pair
    which, low = where
    for side in (0, 1):
        half = jnp.where(core == side, mine, theirs).astype(jnp.float32)
        result = lax.dynamic_update_slice(result, half[None], (which, low, side * half.shape[1]))
    return result


def on_device(n, groups, hidden, gain, cotangent, blocks, loss_mask, wi_gate, wi_up, wo_weight):
    _, micro_count, row_count, cols = hidden.shape
    position = lax.iota(jnp.int32, row_count)
    offset = position % TLEN
    sequence = position // TLEN
    picker = (sequence[None, :] == lax.iota(jnp.int32, blocks.shape[2])[:, None]).astype(jnp.int32)
    limit_pos = jnp.sum(blocks[0][:, :, None] * picker[None, :, :], axis=1) * BLOCK
    weight = (offset[None, :] < limit_pos).astype(jnp.int32) * loss_mask[0]
    mine = (lax.iota(jnp.int32, groups) == lax.axis_index("dp")).astype(jnp.int32)
    counts = lax.psum(jnp.sum(weight) * mine, "dp")
    denominator = jnp.maximum(jnp.sum(counts), 1).astype(jnp.float32)
    room = row_count * 3 // 4
    weights = (wi_gate, wi_up, wo_weight)

    def packed(_):
        lines = weight.reshape(-1, 128)
        lane = lax.iota(jnp.int32, 128)
        within = jnp.sum(lines[:, :, None] * (lane[:, None] < lane[None, :]), axis=1)
        line = lax.iota(jnp.int32, lines.shape[0])
        before = jnp.sum(jnp.sum(lines, axis=1)[:, None] * (line[:, None] < line[None, :]), axis=0)
        target = jnp.where(lines > 0, within + before[:, None], -1).reshape(-1)
        pick = (lax.iota(jnp.int32, micro_count * room)[:, None] == target[None, :]).astype(jnp.bfloat16)
        both = [
            jnp.dot(pick, a[0].reshape(-1, cols), preferred_element_type=jnp.float32).astype(a.dtype).reshape(micro_count, room, cols)
            for a in (hidden, cotangent)
        ]
        return gradients(n, groups, 1, *both, gain, denominator, *weights)

    def whole(_):
        tangent = cotangent[0] * weight[:, :, None].astype(jnp.bfloat16)
        return gradients(n, groups, 0, hidden[0], tangent, gain, denominator, *weights)

    return lax.cond(jnp.max(counts) <= micro_count * room, packed, whole, 0)


def solution(mesh):
    return jax.shard_map(
        functools.partial(on_device, mesh.shape["mp"], mesh.shape["dp"]),
        mesh=mesh,
        in_specs=(
            P("dp", None, None, "mp"),
            P("mp"),
            P("dp", None, None, "mp"),
            P("dp", None, None),
            P("dp", None, None),
            P("mp", None),
            P("mp", None),
            P("mp", None),
        ),
        out_specs=P(None, "mp", None),
        check_vma=False,
    )
```

```python
import functools

import jax
import jax.numpy as jnp
from jax import lax
from jax.experimental import pallas as pl
from jax.experimental.pallas import tpu as pltpu
from jax.sharding import PartitionSpec as P

BLOCK = 128
TLEN = 256
MESH = pl.DeviceIdType.MESH


def ring_index(place, n):
    back = place // (n // 2)
    return (1 - back) * (2 * place) + back * (2 * (n - 1 - place) + 1)


def ring_place(index, n):
    odd = index % 2
    return (1 - odd) * (index // 2) + odd * (n - 1 - index // 2)


def gather_kernel(n, wide, h_ref, t_ref, g_ref, hg_ref, tg_ref, gg_ref, local_sem, send_sem, recv_sem, gain_sem):
    micro, rows, cols = h_ref.shape
    me = lax.axis_index("mp")
    place = ring_place(me, n)
    ahead = ring_index(lax.rem(place + 1, n), n)
    behind = ring_index(lax.rem(place + n - 1, n), n)

    def spot(ref, owner, m):
        if wide:
            return ref.at[m, :, pl.ds(pl.multiple_of(owner * cols, cols), cols)]
        return ref.at[owner, m]

    barrier = pltpu.get_barrier_semaphore()
    for peer in (ahead, behind):
        pl.semaphore_signal(barrier, inc=1, device_id={"mp": peer}, device_id_type=MESH)
    pl.semaphore_wait(barrier, 2)

    own = []
    copies = {}
    for step in range(n - 1):
        owner = ring_index(lax.rem(place - step + n, n), n)
        if step > 0:
            copies[step - 1, 0, 2].wait_recv()
        copies[step, 0, 2] = pltpu.make_async_remote_copy(
            src_ref=g_ref if step == 0 else gg_ref.at[owner],
            dst_ref=gg_ref.at[owner],
            send_sem=gain_sem.at[1, step],
            recv_sem=gain_sem.at[2, step],
            device_id={"mp": ahead},
            device_id_type=MESH,
        )
        copies[step, 0, 2].start()
        for m in range(micro):
            for way, (src, dst, peer, sign) in enumerate(((h_ref, hg_ref, ahead, -1), (t_ref, tg_ref, behind, 1))):
                owner = ring_index(lax.rem(place + sign * step + n, n), n)
                if step > 0:
                    copies[step - 1, m, way].wait_recv()
                copy = pltpu.make_async_remote_copy(
                    src_ref=src.at[m] if step == 0 else spot(dst, owner, m),
                    dst_ref=spot(dst, owner, m),
                    send_sem=send_sem.at[way, step, m],
                    recv_sem=recv_sem.at[way, step, m],
                    device_id={"mp": peer},
                    device_id_type=MESH,
                )
                copy.start()
                copies[step, m, way] = copy
        if step == 0:
            own.append(pltpu.make_async_copy(g_ref, gg_ref.at[me], gain_sem.at[0, 0]))
            for m in range(micro):
                for way, (src, dst) in enumerate(((h_ref, hg_ref), (t_ref, tg_ref))):
                    own.append(pltpu.make_async_copy(src.at[m], spot(dst, me, m), local_sem.at[way, m]))
            for keep in own:
                keep.start()
    for (step, m, way), copy in copies.items():
        copy.wait_send()
        if step == n - 2:
            copy.wait_recv()
    for keep in own:
        keep.wait()


def gather_rows(hidden, tangent, gain, n, ident):
    micro, rows, cols = hidden.shape
    wide = cols % 128 == 0
    shape = (micro, rows, n * cols) if wide else (n, micro, rows, cols)
    hg, tg, gg = pl.pallas_call(
        functools.partial(gather_kernel, n, wide),
        out_shape=[jax.ShapeDtypeStruct(shape, hidden.dtype)] * 2 + [jax.ShapeDtypeStruct((n, 1, cols), gain.dtype)],
        in_specs=[pl.BlockSpec(memory_space=pl.ANY)] * 3,
        out_specs=[pl.BlockSpec(memory_space=pl.ANY)] * 3,
        scratch_shapes=[
            pltpu.SemaphoreType.DMA((2, micro)),
            pltpu.SemaphoreType.DMA((2, n - 1, micro)),
            pltpu.SemaphoreType.DMA((2, n - 1, micro)),
            pltpu.SemaphoreType.DMA((3, n - 1)),
        ],
        compiler_params=pltpu.CompilerParams(collective_id=ident, has_side_effects=True),
        name=f"gather_rows_{ident}",
    )(hidden, tangent, gain[None])
    if not wide:
        hg, tg = (jnp.transpose(a, (1, 2, 0, 3)).reshape(micro, rows, n * cols) for a in (hg, tg))
    return hg, tg, gg.reshape(n * cols)


def gelu_tanh(value):
    return jax.nn.gelu(value, approximate=True)


def rows_product(rows, units):
    return lax.dot_general(rows, units, (((1,), (1,)), ((), ())), preferred_element_type=jnp.float32)


def kahan(pairs):
    dims = (((0,), (0,)), ((), ()))
    total = comp = None
    for left, right in pairs:
        term = lax.dot_general(left, right, dims, preferred_element_type=jnp.float32)
        if total is None:
            total, comp = term, jnp.zeros_like(term)
            continue
        adjusted = term - comp
        running = total + adjusted
        comp = running - total - adjusted
        total = running
    return total


def swap(value, bit, size):
    return lax.ppermute(value, "dp", [(i, i ^ bit) for i in range(size)])


def core_halves(total):
    core = lax.axis_index("dp") % 2
    half = total.shape[1] // 2
    give = lax.dynamic_slice_in_dim(total, (1 - core) * half, half, 1).astype(jnp.bfloat16)
    keep = lax.dynamic_slice_in_dim(total, core * half, half, 1)
    return give, keep


def over_groups(mine, size):
    bit = 2
    while bit * 2 < size:
        mine = (mine.astype(jnp.float32) + swap(mine, bit, size).astype(jnp.float32)).astype(jnp.bfloat16)
        bit *= 2
    return mine, swap(mine, bit, size)


def gradients(n, groups, ident, hidden, tangent, gain, denominator, wi_gate, wi_up, wo_weight):
    states, whole_tangent, whole_gain = gather_rows(hidden, tangent, gain, n, ident)
    states = states.astype(jnp.float32)
    squares = jnp.mean(states * states, axis=-1, keepdims=True)
    normed = (states * lax.rsqrt(squares + 1e-06) * whole_gain).astype(jnp.bfloat16)
    steps = range(hidden.shape[0])
    units = wi_gate.shape[0]
    middle = (units // 128 + 1) // 2 * 128
    cuts = [0, middle, units] if 0 < middle < units else [0, units]
    sent, spots = [], []

    def job(which, low, lefts, rights, after):
        if after < len(sent):
            lefts, sent[after] = lax.optimization_barrier((lefts, sent[after]))
        else:
            lefts = lax.optimization_barrier(lefts)
        give, keep = core_halves(kahan(list(zip(lefts, rights))))
        sent.append((keep + swap(give, 1, groups).astype(jnp.float32)).astype(jnp.bfloat16))
        spots.append((which, low))
        return give

    normed = [normed[m] for m in steps]
    masked = [whole_tangent[m] for m in steps]
    for low, high in zip(cuts[:-1], cuts[1:]):
        gate_rows, up_rows, out_rows = (w[low:high] for w in (wi_gate, wi_up, wo_weight))
        if sent:
            gate_rows, up_rows, sent[-2] = lax.optimization_barrier((gate_rows, up_rows, sent[-2]))
        up_pre = [rows_product(normed[m], up_rows) for m in steps]
        pulls = [jax.vjp(gelu_tanh, rows_product(normed[m], gate_rows)) for m in steps]
        inner = [(pulls[m][0] * up_pre[m]).astype(jnp.bfloat16) for m in steps]
        give = job(2, low, inner, masked, max(len(sent) - 2, 0))
        out_rows, _ = lax.optimization_barrier((out_rows, give))
        back_grad = [rows_product(masked[m], out_rows) for m in steps]
        grad_up = [(back_grad[m] * pulls[m][0]).astype(jnp.bfloat16) for m in steps]
        job(1, low, grad_up, normed, len(sent) - 1)
        grad_gate = [pulls[m][1](back_grad[m] * up_pre[m])[0].astype(jnp.bfloat16) for m in steps]
        job(0, low, grad_gate, normed, len(sent) - 2)
    result = jnp.zeros((3,) + wi_gate.shape, jnp.float32)
    result, sent[-1] = lax.optimization_barrier((result, sent[-1]))
    core = lax.axis_index("dp") % 2
    crossing = [over_groups(mine, groups) for mine in sent]
    done = []
    for spot, (mine, other) in enumerate(crossing):
        if spot >= 2:
            result = place_halves(result, done[spot - 2], spots[spot - 2], core)
            result, other = lax.optimization_barrier((result, other))
        mine = ((mine.astype(jnp.float32) + other.astype(jnp.float32)) / denominator).astype(jnp.bfloat16)
        done.append((mine, swap(mine, 1, groups)))
    for pair, where in list(zip(done, spots))[-2:]:
        result = place_halves(result, pair, where, core)
    return result


def place_halves(result, pair, where, core):
    mine, theirs = pair
    which, low = where
    for side in (0, 1):
        half = jnp.where(core == side, mine, theirs).astype(jnp.float32)
        result = lax.dynamic_update_slice(result, half[None], (which, low, side * half.shape[1]))
    return result


def on_device(n, groups, hidden, gain, cotangent, blocks, loss_mask, wi_gate, wi_up, wo_weight):
    _, micro_count, row_count, cols = hidden.shape
    position = lax.iota(jnp.int32, row_count)
    offset = position % TLEN
    sequence = position // TLEN
    picker = (sequence[None, :] == lax.iota(jnp.int32, blocks.shape[2])[:, None]).astype(jnp.int32)
    limit_pos = jnp.sum(blocks[0][:, :, None] * picker[None, :, :], axis=1) * BLOCK
    weight = (offset[None, :] < limit_pos).astype(jnp.int32) * loss_mask[0]
    mine = (lax.iota(jnp.int32, groups) == lax.axis_index("dp")).astype(jnp.int32)
    counts = lax.psum(jnp.sum(weight) * mine, "dp")
    denominator = jnp.maximum(jnp.sum(counts), 1).astype(jnp.float32)
    room = row_count * 3 // 4
    weights = (wi_gate, wi_up, wo_weight)

    def packed(_):
        lines = weight.reshape(-1, 128)
        lane = lax.iota(jnp.int32, 128)
        within = jnp.sum(lines[:, :, None] * (lane[:, None] < lane[None, :]), axis=1)
        line = lax.iota(jnp.int32, lines.shape[0])
        before = jnp.sum(jnp.sum(lines, axis=1)[:, None] * (line[:, None] < line[None, :]), axis=0)
        target = jnp.where(lines > 0, within + before[:, None], -1).reshape(-1)
        pick = (lax.iota(jnp.int32, micro_count * room)[:, None] == target[None, :]).astype(jnp.bfloat16)
        both = [
            jnp.dot(pick, a[0].reshape(-1, cols), preferred_element_type=jnp.float32).astype(a.dtype).reshape(micro_count, room, cols)
            for a in (hidden, cotangent)
        ]
        return gradients(n, groups, 1, *both, gain, denominator, *weights)

    def whole(_):
        tangent = cotangent[0] * weight[:, :, None].astype(jnp.bfloat16)
        return gradients(n, groups, 0, hidden[0], tangent, gain, denominator, *weights)

    return lax.cond(jnp.max(counts) <= micro_count * room, packed, whole, 0)


def solution(mesh):
    return jax.shard_map(
        functools.partial(on_device, mesh.shape["mp"], mesh.shape["dp"]),
        mesh=mesh,
        in_specs=(
            P("dp", None, None, "mp"),
            P("mp"),
            P("dp", None, None, "mp"),
            P("dp", None, None),
            P("dp", None, None),
            P("mp", None),
            P("mp", None),
            P("mp", None),
        ),
        out_specs=P(None, "mp", None),
        check_vma=False,
    )
```
